32 devices in a mesh: fsdp: 4 (over y, x), tensor: 8 (over z, core).
Axes of the slice: x: 2, y: 2, z: 4, core: 2. Of those that a mesh axis runs over, the one named last changes fastest.
Arguments:
- inputs_roll: bfloat16 [1536, 4096], P('fsdp', 'tensor'), may hold values from -6 to 6
- cotangent_roll: bfloat16 [1536, 4096], P('fsdp', 'tensor'), may hold values from -0.59765625 to 0.59765625
- counts: int32 [4, 4], P('fsdp'), may hold values from 1 to 3, as said below
- w_gate: bfloat16 [4096, 16384], P('fsdp', 'tensor'), may hold values from -0.09375 to 0.09375
- w_up: bfloat16 [4096, 16384], P('fsdp', 'tensor'), may hold values from -0.09375 to 0.09375
- w_down: bfloat16 [16384, 4096], P('tensor', 'fsdp'), may hold values from -0.046875 to 0.046875
Outputs:
- grad_inputs: bfloat16 [2304, 4096], P('fsdp', 'tensor')
- grad_gate: bfloat16 [4096, 16384], P('fsdp', 'tensor')
- grad_up: bfloat16 [4096, 16384], P('fsdp', 'tensor')
- grad_down: bfloat16 [16384, 4096], P('tensor', 'fsdp')
The draws below stay inside these ranges and needn't reach their ends.
Inputs may be any that keep to these rules, and one draw needn't show every extreme that they name: Row s of counts splits rollout shard s's 8 blocks among the learner shards, in order of learner; every row sums to 8.
All inputs are finite; a program needn't handle non-finite values.
Results may differ from the reference program's by a relative error of at most 0.015.
Values may be sent and summed in bfloat16 or wider, within the bound.
No kernel may reach another device: no remote copies, remote signals or barrier semaphores. Data moves between devices by JAX's collectives and lax.ppermute only.
A program may use at most 128 MiB of HBM per device.

```python
import jax
import jax.numpy as jnp

D = 4096
FF = 16384
BLOCK = 48
SHARE = 2
MOST = 3
KEEP = 8
ROLL_ROWS = 1536
N_FSDP = 4


def draw_counts(key, part):
    key_popular, key_jitter, key_swaps = jax.random.split(jax.random.fold_in(key, 11), 3)
    popular = jax.random.randint(key_popular, (N_FSDP,), 0, 2)
    jitter = jax.random.randint(key_jitter, (N_FSDP, N_FSDP), 0, N_FSDP)
    scores = (jitter + N_FSDP * popular[None, :]) * N_FSDP + jnp.arange(N_FSDP)[None, :]
    ranking = jnp.argsort(-scores, axis=1)
    swaps_count = jax.random.randint(key_swaps, (N_FSDP, 1), 1, N_FSDP // 2 + 1)
    positions = jnp.arange(N_FSDP)[None, :]
    amounts = SHARE + (positions < swaps_count).astype(jnp.int32) - (positions >= N_FSDP - swaps_count).astype(jnp.int32)
    sources = jnp.broadcast_to(jnp.arange(N_FSDP)[:, None], (N_FSDP, N_FSDP))
    return jnp.zeros((N_FSDP, N_FSDP), jnp.int32).at[sources, ranking].set(amounts.astype(jnp.int32))


def levels(own_key, extent, shards, smallest, top_value):
    def one(axis_at, parts):
        heights = jax.random.uniform(jax.random.fold_in(jax.random.fold_in(own_key, 6), axis_at), (parts,), jnp.float32, smallest / len(shards), top_value / len(shards))
        return jnp.repeat(jnp.exp(heights), extent[axis_at] // parts).reshape((-1,) + (1,) * (len(extent) - axis_at - 1))

    loudness = one(*shards[0])
    for cut in shards[1:]:
        loudness = loudness * one(*cut)
    return loudness


def normal_values(stream_key, dims, spread, most, shards=(), kind=jnp.bfloat16):
    values = spread * jax.random.normal(stream_key, dims, jnp.float32)
    if shards:
        values = values * levels(stream_key, dims, shards, -0.22, 0.18)
    return jnp.clip(values, -most, most).astype(kind)


def setup_inputs(seed: int = 0) -> dict:
    seeds = jax.random.split(jax.random.key(seed), 7)
    return {
        "inputs_roll": normal_values(seeds[0], (ROLL_ROWS, D), 1.0, 6.0, ((0, 4), (1, 8))),
        "cotangent_roll": normal_values(seeds[1], (ROLL_ROWS, D), 0.1, 0.59765625, ((0, 4), (1, 8))),
        "counts": draw_counts(jax.random.fold_in(seeds[6], 71), 0),
        "w_gate": normal_values(seeds[3], (D, FF), D ** -0.5, 0.09375, ((0, 4), (1, 8))),
        "w_up": normal_values(seeds[4], (D, FF), D ** -0.5, 0.09375, ((0, 4), (1, 8))),
        "w_down": normal_values(seeds[5], (FF, D), FF ** -0.5, 0.046875, ((0, 8), (1, 4))),
    }


def route_blocks(blocks, counts):
    offsets = jnp.cumsum(counts, axis=1) - counts
    slot_ids = jnp.arange(MOST, dtype=jnp.int32)
    chosen = offsets.T[:, :, None] + slot_ids[None, None, :]
    is_live = slot_ids[None, None, :] < counts.T[:, :, None]
    chosen = jnp.where(is_live, chosen, 0).astype(jnp.int32)
    sources = jnp.broadcast_to(jnp.arange(N_FSDP, dtype=jnp.int32)[None, :, None], chosen.shape)
    picked = blocks[sources, chosen]
    picked = jnp.where(is_live[:, :, :, None, None], picked, jnp.zeros_like(picked))
    return picked.reshape(N_FSDP * N_FSDP * MOST * BLOCK, blocks.shape[-1])


def reference(inputs_roll, cotangent_roll, counts, w_gate, w_up, w_down):
    features = inputs_roll.shape[1]
    inputs = route_blocks(inputs_roll.reshape(N_FSDP, KEEP, BLOCK, features), counts)
    cotangent = route_blocks(cotangent_roll.reshape(N_FSDP, KEEP, BLOCK, features), counts)
    gate_act = jnp.dot(inputs, w_gate, preferred_element_type=jnp.float32)
    up_act = jnp.dot(inputs, w_up, preferred_element_type=jnp.float32)
    sigmoid_gate = jax.nn.sigmoid(gate_act)
    silu_gate = gate_act * sigmoid_gate
    hidden = (silu_gate * up_act).astype(jnp.bfloat16)
    grad_hidden = jnp.dot(cotangent, w_down.T, preferred_element_type=jnp.float32)
    grad_gate_pre = (grad_hidden * up_act * sigmoid_gate * (1.0 + gate_act * (1.0 - sigmoid_gate))).astype(jnp.bfloat16)
    grad_up_pre = (grad_hidden * silu_gate).astype(jnp.bfloat16)
    grad_inputs = (jnp.dot(grad_gate_pre, w_gate.T, preferred_element_type=jnp.float32)
                   + jnp.dot(grad_up_pre, w_up.T, preferred_element_type=jnp.float32)).astype(jnp.bfloat16)
    grad_gate = jnp.dot(inputs.T, grad_gate_pre, preferred_element_type=jnp.float32).astype(jnp.bfloat16)
    grad_up = jnp.dot(inputs.T, grad_up_pre, preferred_element_type=jnp.float32).astype(jnp.bfloat16)
    grad_down = jnp.dot(hidden.T, cotangent, preferred_element_type=jnp.float32).astype(jnp.bfloat16)
    return (grad_inputs, grad_gate, grad_up, grad_down)
```

```python
import jax
import jax.numpy as jnp
from jax import lax
from jax.sharding import PartitionSpec as P

BLOCK = 48
MOST = 3


def swap(values, offset):
    size = lax.axis_size("fsdp")
    return lax.ppermute(values, "fsdp", [(i, i ^ offset) for i in range(size)])


def matmul(left_side, right_side):
    return jnp.dot(left_side, right_side, preferred_element_type=jnp.float32)


def matmul_t(left_side, right_side):
    return lax.dot_general(
        left_side, right_side, (((1,), (1,)), ((), ())), preferred_element_type=jnp.float32
    )


def contract_rows(left_side, right_side):
    return lax.dot_general(
        left_side, right_side, (((0,), (0,)), ((), ())), preferred_element_type=jnp.float32
    )


def spread_rows(rows):
    size = lax.axis_size("fsdp")
    me = lax.axis_index("fsdp")
    own_rows = lax.all_to_all(rows, "tensor", split_axis=0, concat_axis=1, tiled=True)
    width = own_rows.shape[1] // size
    got = {}
    for k in (3, 1, 2, 0):
        piece = lax.dynamic_slice_in_dim(own_rows, (me ^ k) * width, width, axis=1)
        if k:
            piece = swap(piece, k)
        got[k] = lax.all_gather(piece, "tensor", axis=0, tiled=True)
    return got


def reduce_blocks(partial, first, second):
    low = jnp.bfloat16
    far = swap(partial[3].astype(low), first)
    near = swap(partial[first].astype(low), first)
    passed = (partial[second] + far.astype(jnp.float32)).astype(low)
    last = swap(passed, second)
    return partial[0] + near.astype(jnp.float32) + last.astype(jnp.float32)


def gather_blocks(own, first, second):
    got = {0: own}
    got[first] = swap(own, first)
    got[second] = swap(own, second)
    got[3] = swap(got[first], second)
    return got


def join(blocks):
    return jnp.concatenate([blocks[k] for k in range(4)], axis=0)


def route(blocks, all_counts):
    shards, kept = blocks.shape[0], blocks.shape[1]
    me = lax.axis_index("fsdp")
    flat = blocks.reshape((shards * kept,) + blocks.shape[2:])
    offsets = jnp.cumsum(all_counts, axis=1) - all_counts
    slot_ids = jnp.arange(MOST, dtype=jnp.int32)
    counts_gs = all_counts.T
    chosen = offsets.T[:, :, None] + slot_ids[None, None, :]
    is_live = slot_ids[None, None, :] < counts_gs[:, :, None]
    start = (me ^ jnp.arange(shards, dtype=jnp.int32)) * kept
    index = jnp.where(is_live, chosen + start[None, :, None], 0)
    picked = jnp.take(flat, index.reshape(-1), axis=0)
    picked = picked.reshape(is_live.shape + blocks.shape[2:])
    return jnp.where(is_live[:, :, :, None, None], picked, jnp.zeros_like(picked))


def per_device(inputs_roll, cotangent_roll, counts, w_gate, w_up, w_down):
    size = lax.axis_size("fsdp")
    wide = lax.axis_size("tensor")
    assert size == 4 and wide % size == 0
    rows = inputs_roll.shape[0]
    depth = w_gate.shape[0]
    all_counts = lax.all_gather(counts, "fsdp", axis=0, tiled=True)

    inputs = spread_rows(inputs_roll)
    cotangent = spread_rows(cotangent_roll)

    order = (3, 1, 2, 0)
    gate_part = {k: matmul(inputs[k], w_gate) for k in order}
    up_part = {k: matmul(inputs[k], w_up) for k in order}
    hidden_part = {k: matmul_t(cotangent[k], w_down) for k in order}

    gate_act = reduce_blocks(gate_part, 1, 2)
    up_act = reduce_blocks(up_part, 2, 1)
    grad_hidden = reduce_blocks(hidden_part, 1, 2)

    sigmoid_gate = jax.nn.sigmoid(gate_act)
    silu_gate = gate_act * sigmoid_gate
    hidden = (silu_gate * up_act).astype(jnp.bfloat16)
    grad_gate_pre = (
        grad_hidden * up_act * sigmoid_gate * (1.0 + gate_act * (1.0 - sigmoid_gate))
    ).astype(jnp.bfloat16)
    grad_up_pre = (grad_hidden * silu_gate).astype(jnp.bfloat16)

    all_up = gather_blocks(grad_up_pre, 1, 2)
    all_gate = gather_blocks(grad_gate_pre, 2, 1)
    all_hidden = gather_blocks(hidden, 1, 2)

    m = wide // size
    width = depth // wide

    def reordered(weight):
        parts = weight.reshape(m, size, width, weight.shape[1])
        return jnp.swapaxes(parts, 0, 1).reshape(weight.shape)

    gate_rows, up_rows = reordered(w_gate), reordered(w_up)
    summed = []
    for k in range(size):
        terms = matmul_t(all_up[k], up_rows) + matmul_t(all_gate[k], gate_rows)
        summed.append(
            lax.psum_scatter(
                terms.astype(jnp.bfloat16), "tensor", scatter_dimension=1, tiled=True
            )
        )
    blocks = jnp.stack(summed).reshape(size, rows // BLOCK, BLOCK, width)
    sent = route(blocks, all_counts).reshape(size, -1, width)
    got = lax.all_to_all(sent, "fsdp", split_axis=0, concat_axis=0, tiled=True)
    place = lax.axis_index("tensor") // m
    turns = []
    for r in range(size):
        chunk = lax.dynamic_index_in_dim(got, (place + r) % size, axis=0, keepdims=False)
        if r:
            ring = [(t, m * ((t // m + r) % size) + t % m) for t in range(wide)]
            chunk = lax.ppermute(chunk, "tensor", ring)
        turns.append(chunk)
    turns = jnp.stack(turns)
    picked = jnp.take(turns, (place - jnp.arange(size)) % size, axis=0)
    grad_inputs = jnp.swapaxes(picked, 0, 1).reshape(picked.shape[1], size * width)

    rows_in, rows_cot = join(inputs), join(cotangent)
    grad_up = contract_rows(rows_in, join(all_up)).astype(jnp.bfloat16)
    grad_gate = contract_rows(rows_in, join(all_gate)).astype(jnp.bfloat16)
    grad_down = contract_rows(join(all_hidden), rows_cot).astype(jnp.bfloat16)
    return (grad_inputs, grad_gate, grad_up, grad_down)


def solution(mesh):
    return jax.shard_map(
        per_device,
        mesh=mesh,
        in_specs=(
            P("fsdp", "tensor"),
            P("fsdp", "tensor"),
            P("fsdp", None),
            P("fsdp", "tensor"),
            P("fsdp", "tensor"),
            P("tensor", "fsdp"),
        ),
        out_specs=(
            P("fsdp", "tensor"),
            P("fsdp", "tensor"),
            P("fsdp", "tensor"),
            P("tensor", "fsdp"),
        ),
        check_vma=False,
    )
```

```python
import jax
import jax.numpy as jnp
from jax import lax
from jax.sharding import PartitionSpec as P

BLOCK = 48
MOST = 3


def swap(values, offset):
    size = lax.axis_size("fsdp")
    return lax.ppermute(values, "fsdp", [(i, i ^ offset) for i in range(size)])


class Grid:
    def __init__(self):
        self.n = lax.axis_size("fsdp")
        self.wide = lax.axis_size("tensor")
        self.m = self.wide // self.n
        assert self.n == 4 and self.wide % self.n == 0
        self.me = lax.axis_index("fsdp")
        here = lax.axis_index("tensor")
        self.line = here // self.m
        self.side = here % self.m

    def shift_line(self, values, r):
        n, m = self.n, self.m
        pairs = [(t, m * ((t // m + r) % n) + t % m) for t in range(self.wide)]
        return lax.ppermute(values, "tensor", pairs)

    def shift_side(self, values, r):
        m = self.m
        pairs = [(t, m * (t // m) + (t % m + r) % m) for t in range(self.wide)]
        return lax.ppermute(values, "tensor", pairs)


def matmul(left_side, right_side):
    return jnp.dot(left_side, right_side, preferred_element_type=jnp.float32)


def matmul_t(left_side, right_side):
    return lax.dot_general(
        left_side, right_side, (((1,), (1,)), ((), ())), preferred_element_type=jnp.float32
    )


def contract_rows(left_side, right_side):
    return lax.dot_general(
        left_side, right_side, (((0,), (0,)), ((), ())), preferred_element_type=jnp.float32
    )


def fence(*values):
    return lax.optimization_barrier(values)


def hand_out(grid, rows):
    n = grid.n
    quarters = rows.reshape(n, rows.shape[0] // n, rows.shape[1])
    turns = []
    for r in range(n):
        quarter = lax.dynamic_index_in_dim(quarters, (grid.line + r) % n, axis=0, keepdims=False)
        turns.append(grid.shift_line(quarter, r) if r else quarter)
    return turns


def to_learner_features(grid, turns):
    turns = jnp.stack(turns)
    piece = {}
    for k in range(grid.n):
        turn = (grid.line - (grid.me ^ k)) % grid.n
        piece[k] = lax.dynamic_index_in_dim(turns, turn, axis=0, keepdims=False)
        if k:
            piece[k] = swap(piece[k], k)
    return piece


def all_places(grid, mine):
    places = [mine] + [grid.shift_line(mine, r) for r in range(1, grid.n)]
    return jnp.stack(places, axis=1)


def all_sides(grid, half):
    m = grid.m
    width = half.shape[-1]
    sides = [half] + [grid.shift_side(half, r) for r in range(1, m)]
    blocks = []
    for i in range(half.shape[0]):
        columns = []
        for c in range(m):
            column = sides[0][i]
            for r in range(1, m):
                column = jnp.where((grid.side - c) % m == r, sides[r][i], column)
            columns.append(column.reshape(-1, width))
        blocks.append(jnp.concatenate(columns, axis=1))
    return blocks


def sum_over_tensor(grid, terms):
    n, m = grid.n, grid.m
    rows, depth = terms.shape
    half = depth // m

    def block(values, i, size):
        return lax.dynamic_slice_in_dim(values, i * size, size, axis=1)

    total = block(terms, grid.side, half).astype(jnp.float32)
    for r in range(1, m):
        sent = block(terms, (grid.side + r) % m, half)
        total = total + grid.shift_side(sent, r).astype(jnp.float32)
    total = low(total)
    width = half // n
    kept = block(total, grid.line, width).astype(jnp.float32).reshape(n, rows // n, width)
    for r in range(1, n):
        sent = block(total, (grid.line + r) % n, width)
        came = grid.shift_line(sent, r).reshape(n, rows // n, width)
        kept = kept + jnp.roll(came, r, axis=0).astype(jnp.float32)
    return low(kept)


def route(grid, blocks, all_counts):
    n = grid.n
    width = blocks.shape[-1]
    per_place = blocks.shape[2] // BLOCK
    flat = blocks.reshape(-1, BLOCK, width)
    offsets = jnp.cumsum(all_counts, axis=1) - all_counts
    slot_ids = jnp.arange(MOST, dtype=jnp.int32)
    chosen = offsets.T[:, :, None] + slot_ids[None, None, :]
    is_live = slot_ids[None, None, :] < all_counts.T[:, :, None]
    shard = (grid.me ^ jnp.arange(n, dtype=jnp.int32))[None, :, None]
    place = (grid.line - chosen // per_place) % n
    index = (shard * n + place) * per_place + chosen % per_place
    index = jnp.where(is_live, index, 0)
    picked = jnp.take(flat, index.reshape(-1), axis=0)
    picked = picked.reshape(is_live.shape + (BLOCK, width))
    return jnp.where(is_live[:, :, :, None, None], picked, jnp.zeros_like(picked))


def return_rows(grid, sent):
    n = grid.n
    got = lax.all_to_all(sent, "fsdp", split_axis=0, concat_axis=0, tiled=True)
    turns = []
    for r in range(n):
        chunk = lax.dynamic_index_in_dim(got, (grid.line + r) % n, axis=0, keepdims=False)
        turns.append(grid.shift_line(chunk, r) if r else chunk)
    columns = []
    for q in range(n):
        column = turns[0]
        for r in range(1, n):
            column = jnp.where((grid.line - q) % n == r, turns[r], column)
        columns.append(column)
    return jnp.concatenate(columns, axis=1)


def low(values):
    return values.astype(jnp.bfloat16)


def plus(mine, came):
    return mine + came.astype(jnp.float32)


def per_device(inputs_roll, cotangent_roll, counts, w_gate, w_up, w_down):
    grid = Grid()
    n = grid.n
    x, y = 1, 2

    turns = hand_out(grid, inputs_roll)
    *turns, cotangent_roll = fence(*turns, cotangent_roll)
    piece = to_learner_features(grid, turns)
    cot_turns = hand_out(grid, cotangent_roll)
    by_offset = jnp.concatenate([counts] + [swap(counts, k) for k in range(1, n)], axis=0)
    all_counts = jnp.take(by_offset, grid.me ^ jnp.arange(n, dtype=jnp.int32), axis=0)
    half3 = all_places(grid, piece[3][None])
    cot_piece = to_learner_features(grid, cot_turns)
    others = jnp.stack([piece[1], piece[2], piece[0]])
    half3, others = fence(half3, others)
    half_others = all_places(grid, others)
    in3 = all_sides(grid, half3)[0]
    g3, u3 = low(matmul(in3, w_gate)), low(matmul(in3, w_up))

    g3_came, u3_came = swap(g3, x), swap(u3, y)
    cot_mine = jnp.stack([cot_piece[3], cot_piece[1], cot_piece[2], cot_piece[0]])
    cot_mine, half_others = fence(cot_mine, half_others)
    cot_half = all_places(grid, cot_mine)
    in1, in2, in0 = all_sides(grid, half_others)
    g1, u2 = low(matmul(in1, w_gate)), low(matmul(in2, w_up))

    g1_came, u2_came = swap(g1, x), swap(u2, y)
    g2, u1 = low(plus(matmul(in2, w_gate), g3_came)), low(plus(matmul(in1, w_up), u3_came))

    g2_came, u1_came = swap(g2, y), swap(u1, x)
    g0, u0 = matmul(in0, w_gate), matmul(in0, w_up)
    cot3, cot1, cot2, cot0 = all_sides(grid, cot_half)
    cut = cot3.shape[0] // 2
    h3a, h3b = low(matmul_t(cot3[:cut], w_down)), low(matmul_t(cot3[cut:], w_down))
    h1a, h2b = low(matmul_t(cot1[:cut], w_down)), low(matmul_t(cot2[cut:], w_down))
    g1_came, u2_came, h3a, h3b, h1a, h2b = fence(g1_came, u2_came, h3a, h3b, h1a, h2b)

    h3a_came, h3b_came = swap(h3a, x), swap(h3b, y)
    h1a_came, h2b_came = swap(h1a, x), swap(h2b, y)
    h2a, h1b = matmul_t(cot2[:cut], w_down), matmul_t(cot1[cut:], w_down)
    h0 = matmul_t(cot0, w_down)

    gate_act = plus(plus(g0, g1_came), g2_came)
    up_act = plus(plus(u0, u2_came), u1_came)
    sigmoid_gate = jax.nn.sigmoid(gate_act)
    silu_gate = gate_act * sigmoid_gate
    hidden = low(silu_gate * up_act)
    hidden1, hidden2 = swap(hidden, x), swap(hidden, y)

    h2a_came = swap(low(plus(h2a, h3a_came)), y)
    h1b_came = swap(low(plus(h1b, h3b_came)), x)

    h2a_came, h1b_came, hidden1, hidden2 = fence(h2a_came, h1b_came, hidden1, hidden2)
    hidden3a, hidden3b = swap(hidden2[:cut], x), swap(hidden1[cut:], y)

    h_first = jnp.concatenate([h1a_came, h1b_came], axis=0)
    h_second = jnp.concatenate([h2a_came, h2b_came], axis=0)
    grad_hidden = plus(plus(h0, h_first), h_second)
    gate0 = low(grad_hidden * up_act * sigmoid_gate * (1.0 + gate_act * (1.0 - sigmoid_gate)))
    up0 = low(grad_hidden * silu_gate)
    gate0, up0 = fence(gate0, up0)
    up1, gate2 = swap(up0, x), swap(gate0, y)

    def input_terms(up_block, gate_block):
        return low(matmul_t(up_block, w_up) + matmul_t(gate_block, w_gate))

    hidden3a, hidden3b, gate0, up0 = fence(hidden3a, hidden3b, gate0, up0)
    gate1, up2 = swap(gate0, x), swap(up0, y)
    terms0 = sum_over_tensor(grid, input_terms(up0, gate0))

    gate3, up3 = swap(gate2, x), swap(up1, y)
    rows_in = jnp.concatenate([in0, in1, in2, in3], axis=0)
    rows_cot = jnp.concatenate([cot0, cot1, cot2, cot3], axis=0)
    all_hidden = jnp.concatenate([hidden, hidden1, hidden2, hidden3a, hidden3b], axis=0)
    all_hidden, gate2, up1 = fence(all_hidden, gate2, up1)
    grad_down = low(contract_rows(all_hidden, rows_cot))
    terms1 = sum_over_tensor(grid, input_terms(up1, gate1))
    terms2 = sum_over_tensor(grid, input_terms(up2, gate2))

    terms3 = input_terms(up3, gate3)
    rows_in, terms3 = fence(rows_in, terms3)
    terms3 = sum_over_tensor(grid, terms3)
    grad_gate = low(contract_rows(rows_in, jnp.concatenate([gate0, gate1, gate2, gate3], axis=0)))
    grad_up = low(contract_rows(rows_in, jnp.concatenate([up0, up1, up2, up3], axis=0)))
    sent = route(grid, jnp.stack([terms0, terms1, terms2, terms3]), all_counts)
    grad_inputs = return_rows(grid, sent.reshape(n, -1, sent.shape[-1]))
    return (grad_inputs, grad_gate, grad_up, grad_down)


def solution(mesh):
    return jax.shard_map(
        per_device,
        mesh=mesh,
        in_specs=(
            P("fsdp", "tensor"),
            P("fsdp", "tensor"),
            P("fsdp", None),
            P("fsdp", "tensor"),
            P("fsdp", "tensor"),
            P("tensor", "fsdp"),
        ),
        out_specs=(
            P("fsdp", "tensor"),
            P("fsdp", "tensor"),
            P("fsdp", "tensor"),
            P("tensor", "fsdp"),
        ),
        check_vma=False,
    )
```

```python
import jax
import jax.numpy as jnp
from jax import lax
from jax.sharding import PartitionSpec as P


BLOCK = 48
MOST = 3


def swap(values, offset):
    size = lax.axis_size("fsdp")
    return lax.ppermute(values, "fsdp", [(i, i ^ offset) for i in range(size)])


class Grid:
    def __init__(self):
        self.n = lax.axis_size("fsdp")
        self.wide = lax.axis_size("tensor")
        self.m = self.wide // self.n
        assert self.n == 4 and self.wide % self.n == 0
        self.me = lax.axis_index("fsdp")
        here = lax.axis_index("tensor")
        self.line = here // self.m
        self.side = here % self.m

    def shift_line(self, values, r):
        n, m = self.n, self.m
        pairs = [(t, m * ((t // m + r) % n) + t % m) for t in range(self.wide)]
        return lax.ppermute(values, "tensor", pairs)

    def shift_side(self, values, r):
        m = self.m
        pairs = [(t, m * (t // m) + (t % m + r) % m) for t in range(self.wide)]
        return lax.ppermute(values, "tensor", pairs)


def matmul(left_side, right_side):
    return jnp.dot(left_side, right_side, preferred_element_type=jnp.float32)


def matmul_t(left_side, right_side):
    return lax.dot_general(
        left_side, right_side, (((1,), (1,)), ((), ())), preferred_element_type=jnp.float32
    )


def contract_rows(left_side, right_side):
    return lax.dot_general(
        left_side, right_side, (((0,), (0,)), ((), ())), preferred_element_type=jnp.float32
    )


def fence(*values):
    return lax.optimization_barrier(values)


def hand_out(grid, rows):
    n = grid.n
    quarters = rows.reshape(n, rows.shape[0] // n, rows.shape[1])
    turns = []
    for r in range(n):
        quarter = lax.dynamic_index_in_dim(quarters, (grid.line + r) % n, axis=0, keepdims=False)
        turns.append(grid.shift_line(quarter, r) if r else quarter)
    return turns


def to_learner_features(grid, turns):
    turns = jnp.stack(turns)
    piece = {}
    for k in range(grid.n):
        turn = (grid.line - (grid.me ^ k)) % grid.n
        piece[k] = lax.dynamic_index_in_dim(turns, turn, axis=0, keepdims=False)
        if k:
            piece[k] = swap(piece[k], k)
    return piece


def all_places(grid, mine):
    places = [mine] + [grid.shift_line(mine, r) for r in range(1, grid.n)]
    return jnp.stack(places, axis=1)


def all_sides(grid, half):
    m = grid.m
    width = half.shape[-1]
    sides = [half] + [grid.shift_side(half, r) for r in range(1, m)]
    blocks = []
    for i in range(half.shape[0]):
        columns = []
        for c in range(m):
            column = sides[0][i]
            for r in range(1, m):
                column = jnp.where((grid.side - c) % m == r, sides[r][i], column)
            columns.append(column.reshape(-1, width))
        blocks.append(jnp.concatenate(columns, axis=1))
    return blocks


def sum_over_tensor(grid, terms):
    n, m = grid.n, grid.m
    blocks, rows, depth = terms.shape
    half = depth // m

    def block(values, i, size):
        return lax.dynamic_slice_in_dim(values, i * size, size, axis=2)

    total = block(terms, grid.side, half).astype(jnp.float32)
    for r in range(1, m):
        sent = block(terms, (grid.side + r) % m, half)
        total = total + grid.shift_side(sent, r).astype(jnp.float32)
    total = low(total)
    width = half // n
    shape = (blocks, n, rows // n, width)
    kept = block(total, grid.line, width).astype(jnp.float32).reshape(shape)
    for r in range(1, n):
        sent = block(total, (grid.line + r) % n, width)
        came = grid.shift_line(sent, r).reshape(shape)
        kept = kept + jnp.roll(came, r, axis=1).astype(jnp.float32)
    return low(kept)


def route(grid, blocks, all_counts):
    n = grid.n
    width = blocks.shape[-1]
    per_place = blocks.shape[2] // BLOCK
    flat = blocks.reshape(-1, BLOCK, width)
    offsets = jnp.cumsum(all_counts, axis=1) - all_counts
    slot_ids = jnp.arange(MOST, dtype=jnp.int32)
    chosen = offsets.T[:, :, None] + slot_ids[None, None, :]
    is_live = slot_ids[None, None, :] < all_counts.T[:, :, None]
    shard = (grid.me ^ jnp.arange(n, dtype=jnp.int32))[None, :, None]
    place = (grid.line - chosen // per_place) % n
    index = (shard * n + place) * per_place + chosen % per_place
    index = jnp.where(is_live, index, 0)
    picked = jnp.take(flat, index.reshape(-1), axis=0)
    picked = picked.reshape(is_live.shape + (BLOCK, width))
    return jnp.where(is_live[:, :, :, None, None], picked, jnp.zeros_like(picked))


def return_rows(grid, sent):
    n = grid.n
    got = lax.all_to_all(sent, "fsdp", split_axis=0, concat_axis=0, tiled=True)
    turns = []
    for r in range(n):
        chunk = lax.dynamic_index_in_dim(got, (grid.line + r) % n, axis=0, keepdims=False)
        turns.append(grid.shift_line(chunk, r) if r else chunk)
    columns = []
    for q in range(n):
        column = turns[0]
        for r in range(1, n):
            column = jnp.where((grid.line - q) % n == r, turns[r], column)
        columns.append(column)
    return jnp.concatenate(columns, axis=1)


def low(values):
    return values.astype(jnp.bfloat16)


def plus(mine, came):
    return mine + came.astype(jnp.float32)


def steps(inputs_roll, cotangent_roll, counts, w_gate, w_up, w_down):
    grid = Grid()
    n = grid.n
    x, y = 1, 2

    def swap_x(values):
        return swap(values, x)

    def swap_y(values):
        return swap(values, y)

    turns = hand_out(grid, inputs_roll)
    *turns, cotangent_roll = fence(*turns, cotangent_roll)
    piece = to_learner_features(grid, turns)
    half3 = all_places(grid, piece[3][None])
    cot_turns = hand_out(grid, cotangent_roll)
    in3 = all_sides(grid, half3)[0]
    g3, u3 = low(matmul(in3, w_gate)), low(matmul(in3, w_up))

    g3_came, u3_came = swap_x(g3), swap_y(u3)
    half_others = all_places(grid, jnp.stack([piece[1], piece[2], piece[0]]))
    cot_piece = to_learner_features(grid, cot_turns)
    in1, in2, in0 = all_sides(grid, half_others)
    g1, u2 = low(matmul(in1, w_gate)), low(matmul(in2, w_up))

    g1_came, u2_came = swap_x(g1), swap_y(u2)
    cot_mine = jnp.stack([cot_piece[3], cot_piece[1], cot_piece[2], cot_piece[0]])
    cot_half = all_places(grid, cot_mine)
    g2, u1 = low(plus(matmul(in2, w_gate), g3_came)), low(plus(matmul(in1, w_up), u3_came))

    g2_came, u1_came = swap_y(g2), swap_x(u1)
    by_offset = jnp.concatenate([counts] + [swap(counts, k) for k in range(1, n)], axis=0)
    all_counts = jnp.take(by_offset, grid.me ^ jnp.arange(n, dtype=jnp.int32), axis=0)
    g0, u0 = matmul(in0, w_gate), matmul(in0, w_up)
    cot3, cot1, cot2, cot0 = all_sides(grid, cot_half)
    cut = cot3.shape[0] // 2
    h3a, h3b = low(matmul_t(cot3[:cut], w_down)), low(matmul_t(cot3[cut:], w_down))
    h1a, h2b = low(matmul_t(cot1[:cut], w_down)), low(matmul_t(cot2[cut:], w_down))
    g1_came, u2_came, h3a, h3b, h1a, h2b = fence(g1_came, u2_came, h3a, h3b, h1a, h2b)

    h3a_came, h3b_came = swap_x(h3a), swap_y(h3b)
    h1a_came, h2b_came = swap_x(h1a), swap_y(h2b)
    h2a, h1b = matmul_t(cot2[:cut], w_down), matmul_t(cot1[cut:], w_down)
    h0 = matmul_t(cot0, w_down)

    gate_act = plus(plus(g0, g1_came), g2_came)
    up_act = plus(plus(u0, u2_came), u1_came)
    sigmoid_gate = jax.nn.sigmoid(gate_act)
    silu_gate = gate_act * sigmoid_gate
    hidden = low(silu_gate * up_act)
    hidden1, hidden2 = swap_x(hidden), swap_y(hidden)

    h2a_came = swap_y(low(plus(h2a, h3a_came)))
    h1b_came = swap_x(low(plus(h1b, h3b_came)))

    h2a_came, h1b_came, hidden1, hidden2 = fence(h2a_came, h1b_came, hidden1, hidden2)
    hidden3a, hidden3b = swap_x(hidden2[:cut]), swap_y(hidden1[cut:])

    h_first = jnp.concatenate([h1a_came, h1b_came], axis=0)
    h_second = jnp.concatenate([h2a_came, h2b_came], axis=0)
    grad_hidden = plus(plus(h0, h_first), h_second)
    gate0 = low(grad_hidden * up_act * sigmoid_gate * (1.0 + gate_act * (1.0 - sigmoid_gate)))
    up0 = low(grad_hidden * silu_gate)
    gate0, up0 = fence(gate0, up0)
    up1, up2 = swap_x(up0), swap_y(up0)

    def input_terms(up_block, gate_block):
        return low(matmul_t(up_block, w_up) + matmul_t(gate_block, w_gate))

    hidden3 = jnp.concatenate([hidden3a, hidden3b], axis=0)
    hidden3, gate0, up0 = fence(hidden3, gate0, up0)
    gate1, gate2 = swap_x(gate0), swap_y(gate0)
    terms0 = input_terms(up0, gate0)
    terms0 = sum_over_tensor(grid, terms0[None])
    rows_in = jnp.concatenate([in0, in1, in2, in3], axis=0)
    rows_cot = jnp.concatenate([cot0, cot1, cot2, cot3], axis=0)
    all_hidden = jnp.concatenate([hidden, hidden1, hidden2, hidden3], axis=0)
    grad_down = low(contract_rows(all_hidden, rows_cot))

    up3a, up3b = swap_x(up2[:cut]), swap_y(up1[cut:])
    up_terms1, up_terms2 = matmul_t(up1, w_up), matmul_t(up2, w_up)
    up_terms1, up_terms2 = fence(up_terms1, up_terms2)
    terms1 = low(up_terms1 + matmul_t(gate1, w_gate))
    terms2 = low(up_terms2 + matmul_t(gate2, w_gate))
    terms12 = sum_over_tensor(grid, jnp.stack([terms1, terms2]))

    gate3a, gate3b = swap_x(gate2[:cut]), swap_y(gate1[cut:])
    (up3,) = fence(jnp.concatenate([up3a, up3b], axis=0))
    grad_up = low(contract_rows(rows_in, jnp.concatenate([up0, up1, up2, up3], axis=0)))

    gate3 = jnp.concatenate([gate3a, gate3b], axis=0)
    (gate3,) = fence(gate3)
    terms3 = sum_over_tensor(grid, input_terms(up3, gate3)[None])
    all_gate = jnp.concatenate([gate0, gate1, gate2, gate3], axis=0)
    grad_gate = low(contract_rows(rows_in, all_gate))
    sent = route(grid, jnp.concatenate([terms0, terms12, terms3], axis=0), all_counts)
    grad_inputs = return_rows(grid, sent.reshape(n, -1, sent.shape[-1]))
    return (grad_inputs, grad_gate, grad_up, grad_down)


def solution(mesh):
    return jax.shard_map(
        steps,
        mesh=mesh,
        in_specs=(
            P("fsdp", "tensor"),
            P("fsdp", "tensor"),
            P("fsdp", None),
            P("fsdp", "tensor"),
            P("fsdp", "tensor"),
            P("tensor", "fsdp"),
        ),
        out_specs=(
            P("fsdp", "tensor"),
            P("fsdp", "tensor"),
            P("fsdp", "tensor"),
            P("tensor", "fsdp"),
        ),
        check_vma=False,
    )
```

```python
import jax
import jax.numpy as jnp
from jax import lax
from jax.sharding import PartitionSpec as P


BLOCK = 48
MOST = 3


def swap(values, offset):
    size = lax.axis_size("fsdp")
    return lax.ppermute(values, "fsdp", [(i, i ^ offset) for i in range(size)])


class Grid:
    def __init__(self):
        self.n = lax.axis_size("fsdp")
        self.wide = lax.axis_size("tensor")
        self.m = self.wide // self.n
        assert self.n == 4 and self.wide % self.n == 0
        self.me = lax.axis_index("fsdp")
        here = lax.axis_index("tensor")
        self.line = here // self.m
        self.side = here % self.m

    def shift_line(self, values, r):
        n, m = self.n, self.m
        pairs = [(t, m * ((t // m + r) % n) + t % m) for t in range(self.wide)]
        return lax.ppermute(values, "tensor", pairs)

    def shift_side(self, values, r):
        m = self.m
        pairs = [(t, m * (t // m) + (t % m + r) % m) for t in range(self.wide)]
        return lax.ppermute(values, "tensor", pairs)


def across(grid, values, target):
    n, m, wide = grid.n, grid.m, grid.wide
    pairs = []
    for f in range(n):
        for t in range(wide):
            to_f, to_line = target(f, t // m)
            pairs.append((f * wide + t, to_f * wide + to_line * m + t % m))
    return lax.ppermute(values, ("fsdp", "tensor"), pairs)


def matmul(left_side, right_side):
    return jnp.dot(left_side, right_side, preferred_element_type=jnp.float32)


def matmul_t(left_side, right_side):
    return lax.dot_general(
        left_side, right_side, (((1,), (1,)), ((), ())), preferred_element_type=jnp.float32
    )


def contract_rows(left_side, right_side):
    return lax.dot_general(
        left_side, right_side, (((0,), (0,)), ((), ())), preferred_element_type=jnp.float32
    )


def fence(*values):
    return lax.optimization_barrier(values)


def hand_out(grid, rows):
    n = grid.n
    quarters = rows.reshape(n, rows.shape[0] // n, rows.shape[1])
    turns = []
    for k in range(n):
        quarter = lax.dynamic_index_in_dim(quarters, (grid.me + k) % n, axis=0, keepdims=False)
        turns.append(across(grid, quarter, lambda f, line, k=k: (line, (f + k) % n)))
    return turns


def by_shard(grid, turns):
    turns = jnp.stack(turns)
    return [
        lax.dynamic_index_in_dim(turns, (grid.line - (grid.me ^ k)) % grid.n, 0, keepdims=False)
        for k in range(grid.n)
    ]


def all_places(grid, mine):
    places = [mine] + [grid.shift_line(mine, r) for r in range(1, grid.n)]
    return jnp.stack(places, axis=1)


def all_sides(grid, half):
    m = grid.m
    width = half.shape[-1]
    sides = [half] + [grid.shift_side(half, r) for r in range(1, m)]
    blocks = []
    for i in range(half.shape[0]):
        columns = []
        for c in range(m):
            column = sides[0][i]
            for r in range(1, m):
                column = jnp.where((grid.side - c) % m == r, sides[r][i], column)
            columns.append(column.reshape(-1, width))
        blocks.append(jnp.concatenate(columns, axis=1))
    return blocks


def sum_over_tensor(grid, terms):
    n, m = grid.n, grid.m
    blocks, rows, depth = terms.shape
    half = depth // m

    def block(values, i, size):
        return lax.dynamic_slice_in_dim(values, i * size, size, axis=2)

    total = block(terms, grid.side, half).astype(jnp.float32)
    for r in range(1, m):
        sent = block(terms, (grid.side + r) % m, half)
        total = total + grid.shift_side(sent, r).astype(jnp.float32)
    total = low(total)
    width = half // n
    shape = (blocks, n, rows // n, width)
    kept = block(total, grid.line, width).astype(jnp.float32).reshape(shape)
    for r in range(1, n):
        sent = block(total, (grid.line + r) % n, width)
        came = grid.shift_line(sent, r).reshape(shape)
        kept = kept + jnp.roll(came, r, axis=1).astype(jnp.float32)
    return low(kept)


def route(grid, blocks, all_counts):
    n = grid.n
    width = blocks.shape[-1]
    per_place = blocks.shape[2] // BLOCK
    flat = blocks.reshape(-1, BLOCK, width)
    offsets = jnp.cumsum(all_counts, axis=1) - all_counts
    slot_ids = jnp.arange(MOST, dtype=jnp.int32)
    chosen = offsets.T[:, :, None] + slot_ids[None, None, :]
    is_live = slot_ids[None, None, :] < all_counts.T[:, :, None]
    shard = (grid.me ^ jnp.arange(n, dtype=jnp.int32))[None, :, None]
    place = (grid.line - chosen // per_place) % n
    index = (shard * n + place) * per_place + chosen % per_place
    index = jnp.where(is_live, index, 0)
    picked = jnp.take(flat, index.reshape(-1), axis=0)
    picked = picked.reshape(is_live.shape + (BLOCK, width))
    return jnp.where(is_live[:, :, :, None, None], picked, jnp.zeros_like(picked))


def return_rows(grid, sent):
    n = grid.n
    got = lax.all_to_all(sent, "fsdp", split_axis=0, concat_axis=0, tiled=True)
    turns = []
    for r in range(n):
        chunk = lax.dynamic_index_in_dim(got, (grid.line + r) % n, axis=0, keepdims=False)
        turns.append(grid.shift_line(chunk, r) if r else chunk)
    columns = []
    for q in range(n):
        column = turns[0]
        for r in range(1, n):
            column = jnp.where((grid.line - q) % n == r, turns[r], column)
        columns.append(column)
    return jnp.concatenate(columns, axis=1)


def low(values):
    return values.astype(jnp.bfloat16)


def plus(mine, came):
    return mine + came.astype(jnp.float32)


def steps(inputs_roll, cotangent_roll, counts, w_gate, w_up, w_down):
    grid = Grid()
    n = grid.n
    x, y = 1, 2

    def swap_x(values):
        return swap(values, x)

    def swap_y(values):
        return swap(values, y)

    turns = hand_out(grid, inputs_roll)
    *turns, cotangent_roll = fence(*turns, cotangent_roll)
    piece = by_shard(grid, turns)
    half3 = all_places(grid, piece[3][None])
    cot_turns = hand_out(grid, cotangent_roll)
    in3 = all_sides(grid, half3)[0]
    g3, u3 = low(matmul(in3, w_gate)), low(matmul(in3, w_up))

    g3_came, u3_came = swap_x(g3), swap_y(u3)
    half_others = all_places(grid, jnp.stack([piece[1], piece[2], piece[0]]))
    cot_piece = by_shard(grid, cot_turns)
    in1, in2, in0 = all_sides(grid, half_others)
    g1, u2 = low(matmul(in1, w_gate)), low(matmul(in2, w_up))

    g1_came, u2_came = swap_x(g1), swap_y(u2)
    cot_mine = jnp.stack([cot_piece[3], cot_piece[1], cot_piece[2], cot_piece[0]])
    cot_half = all_places(grid, cot_mine)
    g2, u1 = low(plus(matmul(in2, w_gate), g3_came)), low(plus(matmul(in1, w_up), u3_came))

    g2_came, u1_came = swap_y(g2), swap_x(u1)
    by_offset = jnp.concatenate([counts] + [swap(counts, k) for k in range(1, n)], axis=0)
    all_counts = jnp.take(by_offset, grid.me ^ jnp.arange(n, dtype=jnp.int32), axis=0)
    g0, u0 = matmul(in0, w_gate), matmul(in0, w_up)
    cot3, cot1, cot2, cot0 = all_sides(grid, cot_half)
    cut = cot3.shape[0] // 2
    h3a, h3b = low(matmul_t(cot3[:cut], w_down)), low(matmul_t(cot3[cut:], w_down))
    h1a, h2b = low(matmul_t(cot1[:cut], w_down)), low(matmul_t(cot2[cut:], w_down))
    g1_came, u2_came, h3a, h3b, h1a, h2b = fence(g1_came, u2_came, h3a, h3b, h1a, h2b)

    h3a_came, h3b_came = swap_x(h3a), swap_y(h3b)
    h1a_came, h2b_came = swap_x(h1a), swap_y(h2b)
    h2a, h1b = matmul_t(cot2[:cut], w_down), matmul_t(cot1[cut:], w_down)
    h0 = matmul_t(cot0, w_down)

    gate_act = plus(plus(g0, g1_came), g2_came)
    up_act = plus(plus(u0, u2_came), u1_came)
    sigmoid_gate = jax.nn.sigmoid(gate_act)
    silu_gate = gate_act * sigmoid_gate
    hidden = low(silu_gate * up_act)
    hidden1, hidden2 = swap_x(hidden), swap_y(hidden)

    h2a_came = swap_y(low(plus(h2a, h3a_came)))
    h1b_came = swap_x(low(plus(h1b, h3b_came)))

    h2a_came, h1b_came, hidden1, hidden2 = fence(h2a_came, h1b_came, hidden1, hidden2)
    hidden3a, hidden3b = swap_x(hidden2[:cut]), swap_y(hidden1[cut:])

    h_first = jnp.concatenate([h1a_came, h1b_came], axis=0)
    h_second = jnp.concatenate([h2a_came, h2b_came], axis=0)
    grad_hidden = plus(plus(h0, h_first), h_second)
    gate0 = low(grad_hidden * up_act * sigmoid_gate * (1.0 + gate_act * (1.0 - sigmoid_gate)))
    up0 = low(grad_hidden * silu_gate)
    gate0, up0 = fence(gate0, up0)
    up1, up2 = swap_x(up0), swap_y(up0)

    def input_terms(up_block, gate_block):
        return low(matmul_t(up_block, w_up) + matmul_t(gate_block, w_gate))

    hidden3 = jnp.concatenate([hidden3a, hidden3b], axis=0)
    hidden3, gate0, up0 = fence(hidden3, gate0, up0)
    gate1, gate2 = swap_x(gate0), swap_y(gate0)
    terms0 = input_terms(up0, gate0)
    terms0 = sum_over_tensor(grid, terms0[None])
    rows_in = jnp.concatenate([in0, in1, in2, in3], axis=0)
    rows_cot = jnp.concatenate([cot0, cot1, cot2, cot3], axis=0)
    all_hidden = jnp.concatenate([hidden, hidden1, hidden2, hidden3], axis=0)
    grad_down = low(contract_rows(all_hidden, rows_cot))

    up3a, up3b = swap_x(up2[:cut]), swap_y(up1[cut:])
    up_terms1, up_terms2 = matmul_t(up1, w_up), matmul_t(up2, w_up)
    up_terms1, up_terms2 = fence(up_terms1, up_terms2)
    terms1 = low(up_terms1 + matmul_t(gate1, w_gate))
    terms2 = low(up_terms2 + matmul_t(gate2, w_gate))
    terms12 = sum_over_tensor(grid, jnp.stack([terms1, terms2]))

    gate3a, gate3b = swap_x(gate2[:cut]), swap_y(gate1[cut:])
    (up3,) = fence(jnp.concatenate([up3a, up3b], axis=0))
    grad_up = low(contract_rows(rows_in, jnp.concatenate([up0, up1, up2, up3], axis=0)))

    gate3 = jnp.concatenate([gate3a, gate3b], axis=0)
    (gate3,) = fence(gate3)
    terms3 = sum_over_tensor(grid, input_terms(up3, gate3)[None])
    all_gate = jnp.concatenate([gate0, gate1, gate2, gate3], axis=0)
    grad_gate = low(contract_rows(rows_in, all_gate))
    sent = route(grid, jnp.concatenate([terms0, terms12, terms3], axis=0), all_counts)
    grad_inputs = return_rows(grid, sent.reshape(n, -1, sent.shape[-1]))
    return (grad_inputs, grad_gate, grad_up, grad_down)


def solution(mesh):
    return jax.shard_map(
        steps,
        mesh=mesh,
        in_specs=(
            P("fsdp", "tensor"),
            P("fsdp", "tensor"),
            P("fsdp", None),
            P("fsdp", "tensor"),
            P("fsdp", "tensor"),
            P("tensor", "fsdp"),
        ),
        out_specs=(
            P("fsdp", "tensor"),
            P("fsdp", "tensor"),
            P("fsdp", "tensor"),
            P("tensor", "fsdp"),
        ),
        check_vma=False,
    )
```

```python
import jax
import jax.numpy as jnp
from jax import lax
from jax.sharding import PartitionSpec as P


BLOCK = 48
MOST = 3


def swap(values, offset):
    size = lax.axis_size("fsdp")
    return lax.ppermute(values, "fsdp", [(i, i ^ offset) for i in range(size)])


class Grid:
    def __init__(self):
        self.n = lax.axis_size("fsdp")
        self.wide = lax.axis_size("tensor")
        self.m = self.wide // self.n
        assert self.n == 4 and self.wide % self.n == 0
        self.me = lax.axis_index("fsdp")
        here = lax.axis_index("tensor")
        self.line = here // self.m
        self.side = here % self.m

    def shift_line(self, values, r):
        n, m = self.n, self.m
        pairs = [(t, m * ((t // m + r) % n) + t % m) for t in range(self.wide)]
        return lax.ppermute(values, "tensor", pairs)

    def shift_side(self, values, r):
        m = self.m
        pairs = [(t, m * (t // m) + (t % m + r) % m) for t in range(self.wide)]
        return lax.ppermute(values, "tensor", pairs)


def across(grid, values, target):
    n, m, wide = grid.n, grid.m, grid.wide
    pairs = []
    for f in range(n):
        for t in range(wide):
            to_f, to_line = target(f, t // m)
            pairs.append((f * wide + t, to_f * wide + to_line * m + t % m))
    return lax.ppermute(values, ("fsdp", "tensor"), pairs)


def matmul(left_side, right_side):
    return jnp.dot(left_side, right_side, preferred_element_type=jnp.float32)


def matmul_t(left_side, right_side):
    return lax.dot_general(
        left_side, right_side, (((1,), (1,)), ((), ())), preferred_element_type=jnp.float32
    )


def contract_rows(left_side, right_side):
    return lax.dot_general(
        left_side, right_side, (((0,), (0,)), ((), ())), preferred_element_type=jnp.float32
    )


def fence(*values):
    return lax.optimization_barrier(values)


def hand_out(grid, rows):
    n = grid.n
    quarters = rows.reshape(n, rows.shape[0] // n, rows.shape[1])
    turns = []
    for k in range(n):
        quarter = lax.dynamic_index_in_dim(quarters, (grid.me + k) % n, axis=0, keepdims=False)
        turns.append(across(grid, quarter, lambda f, line, k=k: (line, (f + k) % n)))
    return turns


def by_shard(grid, turns):
    turns = jnp.stack(turns)
    return [
        lax.dynamic_index_in_dim(turns, (grid.line - (grid.me ^ k)) % grid.n, 0, keepdims=False)
        for k in range(grid.n)
    ]


def all_places(grid, mine):
    places = [mine] + [grid.shift_line(mine, r) for r in range(1, grid.n)]
    return jnp.stack(places, axis=1)


def all_sides(grid, half):
    m = grid.m
    width = half.shape[-1]
    sides = [half] + [grid.shift_side(half, r) for r in range(1, m)]
    blocks = []
    for i in range(half.shape[0]):
        columns = []
        for c in range(m):
            column = sides[0][i]
            for r in range(1, m):
                column = jnp.where((grid.side - c) % m == r, sides[r][i], column)
            columns.append(column.reshape(-1, width))
        blocks.append(jnp.concatenate(columns, axis=1))
    return blocks


def sum_over_tensor(grid, terms):
    n, m = grid.n, grid.m
    blocks, rows, depth = terms.shape
    half = depth // m

    def block(values, i, size):
        return lax.dynamic_slice_in_dim(values, i * size, size, axis=2)

    total = block(terms, grid.side, half).astype(jnp.float32)
    for r in range(1, m):
        sent = block(terms, (grid.side + r) % m, half)
        total = total + grid.shift_side(sent, r).astype(jnp.float32)
    total = low(total)
    width = half // n
    shape = (blocks, n, rows // n, width)
    kept = block(total, grid.line, width).astype(jnp.float32).reshape(shape)
    for r in range(1, n):
        sent = block(total, (grid.line + r) % n, width)
        came = grid.shift_line(sent, r).reshape(shape)
        kept = kept + jnp.roll(came, r, axis=1).astype(jnp.float32)
    return low(kept)


def route(grid, blocks, all_counts):
    n = grid.n
    width = blocks.shape[-1]
    per_place = blocks.shape[2] // BLOCK
    flat = blocks.reshape(-1, BLOCK, width)
    offsets = jnp.cumsum(all_counts, axis=1) - all_counts
    slot_ids = jnp.arange(MOST, dtype=jnp.int32)
    chosen = offsets.T[:, :, None] + slot_ids[None, None, :]
    is_live = slot_ids[None, None, :] < all_counts.T[:, :, None]
    shard = (grid.me ^ jnp.arange(n, dtype=jnp.int32))[None, :, None]
    place = (grid.line - chosen // per_place) % n
    index = (shard * n + place) * per_place + chosen % per_place
    index = jnp.where(is_live, index, 0)
    picked = jnp.take(flat, index.reshape(-1), axis=0)
    picked = picked.reshape(is_live.shape + (BLOCK, width))
    return jnp.where(is_live[:, :, :, None, None], picked, jnp.zeros_like(picked))


def return_rows(grid, sent):
    n = grid.n
    got = lax.all_to_all(sent, "fsdp", split_axis=0, concat_axis=0, tiled=True)
    turns = []
    for r in range(n):
        chunk = lax.dynamic_index_in_dim(got, (grid.line + r) % n, axis=0, keepdims=False)
        turns.append(grid.shift_line(chunk, r) if r else chunk)
    columns = []
    for q in range(n):
        column = turns[0]
        for r in range(1, n):
            column = jnp.where((grid.line - q) % n == r, turns[r], column)
        columns.append(column)
    return jnp.concatenate(columns, axis=1)


def low(values):
    return values.astype(jnp.bfloat16)


def plus(mine, came):
    return mine + came.astype(jnp.float32)


def steps(inputs_roll, cotangent_roll, counts, w_gate, w_up, w_down):
    grid = Grid()
    n = grid.n
    x, y = 1, 2

    def swap_x(values):
        return swap(values, x)

    def swap_y(values):
        return swap(values, y)

    turns = hand_out(grid, inputs_roll)
    *turns, cotangent_roll = fence(*turns, cotangent_roll)
    piece = by_shard(grid, turns)
    half3 = all_places(grid, piece[3][None])
    cot_turns = hand_out(grid, cotangent_roll)
    in3 = all_sides(grid, half3)[0]
    g3, u3 = low(matmul(in3, w_gate)), low(matmul(in3, w_up))

    g3_came, u3_came = swap_x(g3), swap_y(u3)
    half_others = all_places(grid, jnp.stack([piece[1], piece[2], piece[0]]))
    cot_piece = by_shard(grid, cot_turns)
    in1, in2, in0 = all_sides(grid, half_others)
    g1, u2 = low(matmul(in1, w_gate)), low(matmul(in2, w_up))

    g1_came, u2_came = swap_x(g1), swap_y(u2)
    cot_mine = jnp.stack([cot_piece[3], cot_piece[1], cot_piece[2], cot_piece[0]])
    cot_half = all_places(grid, cot_mine)
    g2, u1 = low(plus(matmul(in2, w_gate), g3_came)), low(plus(matmul(in1, w_up), u3_came))

    g2_came, u1_came = swap_y(g2), swap_x(u1)
    by_offset = jnp.concatenate([counts] + [swap(counts, k) for k in range(1, n)], axis=0)
    all_counts = jnp.take(by_offset, grid.me ^ jnp.arange(n, dtype=jnp.int32), axis=0)
    g0, u0 = matmul(in0, w_gate), matmul(in0, w_up)
    cot3, cot1, cot2, cot0 = all_sides(grid, cot_half)
    cut = cot3.shape[0] // 2
    h3a, h3b = low(matmul_t(cot3[:cut], w_down)), low(matmul_t(cot3[cut:], w_down))
    h1a, h2b = low(matmul_t(cot1[:cut], w_down)), low(matmul_t(cot2[cut:], w_down))
    g1_came, u2_came, h3a, h3b, h1a, h2b = fence(g1_came, u2_came, h3a, h3b, h1a, h2b)

    h3a_came, h3b_came = swap_x(h3a), swap_y(h3b)
    h1a_came, h2b_came = swap_x(h1a), swap_y(h2b)
    h2a, h1b = matmul_t(cot2[:cut], w_down), matmul_t(cot1[cut:], w_down)
    h0 = matmul_t(cot0, w_down)

    gate_act = plus(plus(g0, g1_came), g2_came)
    up_act = plus(plus(u0, u2_came), u1_came)
    sigmoid_gate = jax.nn.sigmoid(gate_act)
    silu_gate = gate_act * sigmoid_gate
    hidden = low(silu_gate * up_act)
    hidden1, hidden2 = swap_x(hidden), swap_y(hidden)

    *in_blocks, _ = fence(in0, in1, in2, in3, hidden)
    *cot_blocks, _ = fence(cot0, cot1, cot2, cot3, hidden)
    rows_in = jnp.concatenate(in_blocks, axis=0)
    rows_cot = jnp.concatenate(cot_blocks, axis=0)
    rows_in, rows_cot = fence(rows_in, rows_cot)

    h2a_came = swap_y(low(plus(h2a, h3a_came)))
    h1b_came = swap_x(low(plus(h1b, h3b_came)))

    h2a_came, h1b_came, hidden1, hidden2 = fence(h2a_came, h1b_came, hidden1, hidden2)
    hidden3a, hidden3b = swap_x(hidden2[:cut]), swap_y(hidden1[cut:])

    h_first = jnp.concatenate([h1a_came, h1b_came], axis=0)
    h_second = jnp.concatenate([h2a_came, h2b_came], axis=0)
    grad_hidden = plus(plus(h0, h_first), h_second)
    gate0 = low(grad_hidden * up_act * sigmoid_gate * (1.0 + gate_act * (1.0 - sigmoid_gate)))
    up0 = low(grad_hidden * silu_gate)
    gate0, up0 = fence(gate0, up0)
    up1, up2 = swap_x(up0), swap_y(up0)

    def input_terms(up_block, gate_block):
        return low(matmul_t(up_block, w_up) + matmul_t(gate_block, w_gate))

    hidden3 = jnp.concatenate([hidden3a, hidden3b], axis=0)
    hidden3, gate0, up0 = fence(hidden3, gate0, up0)
    gate1, gate2 = swap_x(gate0), swap_y(gate0)
    terms0 = input_terms(up0, gate0)
    terms0 = sum_over_tensor(grid, terms0[None])
    all_hidden = jnp.concatenate([hidden, hidden1, hidden2, hidden3], axis=0)
    grad_down = low(contract_rows(all_hidden, rows_cot))

    up3a, up3b = swap_x(up2[:cut]), swap_y(up1[cut:])
    up_terms1, up_terms2 = matmul_t(up1, w_up), matmul_t(up2, w_up)
    up_terms1, up_terms2 = fence(up_terms1, up_terms2)
    terms1 = low(up_terms1 + matmul_t(gate1, w_gate))
    terms2 = low(up_terms2 + matmul_t(gate2, w_gate))
    terms12 = sum_over_tensor(grid, jnp.stack([terms1, terms2]))

    gate3a, gate3b = swap_x(gate2[:cut]), swap_y(gate1[cut:])
    (up3,) = fence(jnp.concatenate([up3a, up3b], axis=0))
    grad_up = low(contract_rows(rows_in, jnp.concatenate([up0, up1, up2, up3], axis=0)))

    gate3 = jnp.concatenate([gate3a, gate3b], axis=0)
    (gate3,) = fence(gate3)
    terms3 = sum_over_tensor(grid, input_terms(up3, gate3)[None])
    all_gate = jnp.concatenate([gate0, gate1, gate2, gate3], axis=0)
    grad_gate = low(contract_rows(rows_in, all_gate))
    sent = route(grid, jnp.concatenate([terms0, terms12, terms3], axis=0), all_counts)
    grad_inputs = return_rows(grid, sent.reshape(n, -1, sent.shape[-1]))
    return (grad_inputs, grad_gate, grad_up, grad_down)


def solution(mesh):
    return jax.shard_map(
        steps,
        mesh=mesh,
        in_specs=(
            P("fsdp", "tensor"),
            P("fsdp", "tensor"),
            P("fsdp", None),
            P("fsdp", "tensor"),
            P("fsdp", "tensor"),
            P("tensor", "fsdp"),
        ),
        out_specs=(
            P("fsdp", "tensor"),
            P("fsdp", "tensor"),
            P("fsdp", "tensor"),
            P("tensor", "fsdp"),
        ),
        check_vma=False,
    )
```
